128 devices in a mesh: mod: 64 (over y, z, x), pair: 2 (over core).
Axes of the slice: x: 4, y: 4, z: 4, core: 2. Of those that a mesh axis runs over, the one named last changes fastest.
Arguments:
- query_grads: bfloat16 [512, 256, 16, 128], P(('mod', 'pair')), may hold values from -24 to 24
- train_grads: bfloat16 [1024, 256, 16, 128], P('pair', 'mod'), may hold values from -6 to 6
- left_basis: bfloat16 [256, 16, 16], P('mod'), may hold values from -1.5 to 1.5
- right_basis: bfloat16 [256, 128, 128], P('mod'), may hold values from -0.5 to 0.5
- eigenvalues: bfloat16 [256, 16, 128], P('mod'), may hold values from 0.0009994507 to 10
- block_rows: int32 [256], P('mod'), may hold values from 0 to 16, as said below
Outputs:
- scores: float32 [512, 1024], P('mod', 'pair')
The draws below stay inside these ranges and needn't reach their ends.
Inputs may be any that keep to these rules, and one draw needn't show every extreme that they name: `block_rows`: owner j of the 64 owners holds slots j * 4 to (j + 1) * 4 - 1; of these the first 1 to 4 are live with 8 to 16 rows each and the rest hold 0; some owner has all 4 slots live and a slot of 16 rows, and some live slot has 8 rows.
All inputs are finite; a program needn't handle non-finite values.
Results may differ from the reference program's by a relative error of at most 0.0047.
Values may be sent and summed in bfloat16 or wider, within the bound.
No kernel may reach another device: no remote copies, remote signals or barrier semaphores. Data moves between devices by JAX's collectives and lax.ppermute only.
A program may use at most 128 MiB of HBM per device.

```python
import math
import jax
import jax.numpy as jnp
from jax import lax

COLS = 128
ROWS = 16
SLOTS = 4
TOTAL_SLOTS = 256
QUERIES = 512
TRAIN = 1024


def draw_block_rows(key, part):
    owners = TOTAL_SLOTS // SLOTS
    keys = jax.random.split(jax.random.fold_in(key, 7), 4)
    counts = jax.random.randint(keys[0], (owners,), 1, SLOTS + 1)
    busiest = jax.random.randint(keys[1], (), 0, owners)
    counts = counts.at[busiest].set(SLOTS)
    widths = jax.random.randint(keys[2], (owners, SLOTS), 8, ROWS + 1)
    narrow = (busiest + 1 + jax.random.randint(keys[3], (), 0, owners - 1)) % owners
    widths = widths.at[busiest, 0].set(ROWS).at[narrow, 0].set(8)
    live = jnp.arange(SLOTS)[None, :] < counts[:, None]
    return jnp.where(live, widths, 0).astype(jnp.int32).reshape(TOTAL_SLOTS)


def strengthened(drawn, key, source, target, parts, factor):
    owner, partner = [(jnp.arange(drawn.shape[axis_at]) // (drawn.shape[axis_at] // parts)).reshape([-1 if axis == axis_at else 1 for axis in range(drawn.ndim)]) for axis_at in (source, target)]
    chosen = jax.random.permutation(key, parts)[partner]
    strong = (owner == chosen) | (owner == (partner + parts // 2) % parts)
    return jnp.where(strong, factor * drawn, drawn)


def block_scale(stream_key, shape, pieces, least, largest):
    def one(axis_at, blocks):
        steps = jax.random.uniform(jax.random.fold_in(jax.random.fold_in(stream_key, 6), axis_at), (blocks,), jnp.float32, least / len(pieces), largest / len(pieces))
        return jnp.repeat(jnp.exp(steps), shape[axis_at] // blocks).reshape((-1,) + (1,) * (len(shape) - axis_at - 1))

    level = one(*pieces[0])
    for cut in pieces[1:]:
        level = level * one(*cut)
    return level


def noise(key, dims, scale, most, shards=(), held_as=jnp.bfloat16):
    values = jax.random.normal(key, dims, jnp.float32) * scale
    if len(shards) > 0:
        values = block_scale(key, dims, shards, -0.22, 0.18) * values
    return jnp.clip(values, min=-most, max=most).astype(held_as)


def bell_draw_with(own_key, shape, spread, limit, pieces, heavy, kind=jnp.bfloat16):
    entries = spread * jax.random.normal(own_key, shape, jnp.float32)
    if pieces:
        entries = entries * block_scale(own_key, shape, pieces, -0.22, 0.18)
    return jnp.clip(strengthened(entries, jax.random.fold_in(own_key, 3), *heavy), -limit, limit).astype(kind)


def setup_inputs(seed: int = 0) -> dict:
    key_of = jax.random.split(jax.random.key(seed), 7)
    query_grads = bell_draw_with(key_of[0], (QUERIES, TOTAL_SLOTS, ROWS, COLS), 1.0, 24.0, ((0, 128),), (1, 0, 128, 5.5))
    train_grads = noise(key_of[1], (TRAIN, TOTAL_SLOTS, ROWS, COLS), 1.0, 6.0, ((0, 2), (1, 64)))
    left_basis = noise(key_of[2], (TOTAL_SLOTS, ROWS, ROWS), ROWS ** -0.5, 1.5, ((0, 64),))
    right_basis = noise(key_of[3], (TOTAL_SLOTS, COLS, COLS), COLS ** -0.5, 0.5, ((0, 64),))
    eigenvalues = jnp.clip(jnp.exp(math.log(10.0) - 9.21089 * jax.random.uniform(key_of[4], (TOTAL_SLOTS, ROWS, COLS), jnp.float32) ** block_scale(key_of[4], (TOTAL_SLOTS, ROWS, COLS), ((0, 64),), -0.2, 0.2)), 0.0009994507, 10.0).astype(jnp.bfloat16)
    block_rows = draw_block_rows(jax.random.fold_in(key_of[6], 71), 0)
    return dict(query_grads=query_grads, train_grads=train_grads, left_basis=left_basis, right_basis=right_basis, eigenvalues=eigenvalues, block_rows=block_rows)


def precondition(grad_slot, left_factor, right_factor, eig_block, live_rows):
    count_n, row_total, col_total = grad_slot.shape
    row_mask = (jnp.arange(row_total) < live_rows).astype(jnp.float32)
    left_masked = (left_factor.astype(jnp.float32) * row_mask[:, None] * row_mask[None, :]).astype(jnp.bfloat16)
    masked_grads = (grad_slot.astype(jnp.float32) * row_mask[None, :, None]).astype(jnp.bfloat16)
    rotated_right = jnp.dot(masked_grads.reshape(count_n * row_total, col_total), right_factor, preferred_element_type=jnp.float32).astype(jnp.bfloat16).reshape(count_n, row_total, col_total)
    rotated = jnp.einsum('ba,nbc->nac', left_masked.astype(jnp.float32), rotated_right.astype(jnp.float32))
    eig_float = eig_block.astype(jnp.float32)
    damping = 0.1 * jnp.sum(eig_float * row_mask[:, None]) / jnp.maximum(live_rows * col_total, 1).astype(jnp.float32)
    scaled = (rotated / (eig_float + damping)).astype(jnp.bfloat16)
    back_right = jnp.dot(scaled.reshape(count_n * row_total, col_total), right_factor.T, preferred_element_type=jnp.float32).astype(jnp.bfloat16).reshape(count_n, row_total, col_total)
    return jnp.einsum('ab,nbc->nac', left_masked.astype(jnp.float32), back_right.astype(jnp.float32)).astype(jnp.bfloat16)

def reference(query_grads, train_grads, left_basis, right_basis, eigenvalues, block_rows):
    query_count = query_grads.shape[0]
    train_count = train_grads.shape[0]
    slot_total = query_grads.shape[1]
    norm_scale = 1.0 / math.sqrt(slot_total * query_grads.shape[2] * query_grads.shape[3])

    def slot_step(slot_index, totals):
        grad_slot = lax.dynamic_index_in_dim(query_grads, slot_index, 1, keepdims=False)
        train_slot = lax.dynamic_index_in_dim(train_grads, slot_index, 1, keepdims=False)
        result = precondition(grad_slot, left_basis[slot_index], right_basis[slot_index], eigenvalues[slot_index], block_rows[slot_index])
        return totals + lax.dot_general(result.reshape(query_count, -1), train_slot.reshape(train_count, -1), (((1,), (1,)), ((), ())), preferred_element_type=jnp.float32)
    totals = lax.fori_loop(0, slot_total, slot_step, jnp.zeros((query_count, train_count), jnp.float32))
    return totals * norm_scale
```

```python
import math

import jax
import jax.numpy as jnp
from jax import lax
from jax.experimental import pallas as pl
from jax.experimental.pallas import tpu as pltpu
from jax.sharding import PartitionSpec as P


GROUP = 16
REFINED = (True, False, True)


def dot(a, b):
    return jnp.dot(a, b, preferred_element_type=jnp.float32)


def dot_by_rows(a, b):
    return lax.dot_general(a, b, (((1,), (1,)), ((), ())), preferred_element_type=jnp.float32)


def halves(value):
    high = value.astype(jnp.bfloat16)
    return high, (value - high.astype(jnp.float32)).astype(jnp.bfloat16)


def mixed_by(matrix, value, refined):
    if not refined:
        return dot(matrix, value.astype(jnp.bfloat16))
    high, low = halves(value)
    return dot(matrix, high) + dot(matrix, low)


def arrange_kernel(in_ref, out_ref, held_ref, in_sem, out_sem):
    queries = range(in_ref.shape[0])
    fetch = [
        pltpu.make_async_copy(in_ref.at[q], held_ref.at[q], in_sem.at[q]) for q in queries
    ]
    place = [
        pltpu.make_async_copy(held_ref.at[q], out_ref.at[:, q], out_sem.at[q]) for q in queries
    ]
    for copy in fetch:
        copy.start()
    for q in queries:
        fetch[q].wait()
        place[q].start()
    for copy in place:
        copy.wait()


def by_owner(query_grads, owners):
    count, slot_total, rows, cols = query_grads.shape
    slots = slot_total // owners
    shape = (count, owners, slots, rows, cols)
    return pl.pallas_call(
        arrange_kernel,
        in_specs=[pl.BlockSpec(memory_space=pl.ANY)],
        out_specs=pl.BlockSpec(memory_space=pl.ANY),
        out_shape=jax.ShapeDtypeStruct((owners, count, slots, rows, cols), query_grads.dtype),
        scratch_shapes=[
            pltpu.VMEM(shape, query_grads.dtype),
            pltpu.SemaphoreType.DMA((count,)),
            pltpu.SemaphoreType.DMA((count,)),
        ],
        name="by_owner",
    )(query_grads.reshape(shape))


def train_kernel(
    live_ref, train_ref, left_ref, right_ref, eig_ref, out_ref, turn_ref, mix_ref, pair_ref, inv_ref
):
    block, rows, cols = train_ref.shape
    span = GROUP * rows
    live = live_ref[pl.program_id(0)]

    @pl.when(live == 0)
    def _():
        out_ref[...] = jnp.zeros_like(out_ref)

    @pl.when(live > 0)
    def _():
        at = lambda shape, axis: lax.broadcasted_iota(jnp.int32, shape, axis)
        square = (rows, rows)
        kept = (at(square, 0) < live) & (at(square, 1) < live)
        left = jnp.where(kept, left_ref[...].astype(jnp.float32), 0.0).astype(jnp.bfloat16)
        tall, big = (span, rows), (span, span)
        ones = lambda mask: mask.astype(jnp.float32).astype(jnp.bfloat16)
        inner = ones(at(tall, 0) % rows == at(tall, 1))
        outer = ones(at(tall, 0) // GROUP == at(tall, 1))
        narrow = lambda value: value.astype(jnp.bfloat16)
        turn = dot_by_rows(narrow(dot_by_rows(inner, left)), inner)
        mix = dot_by_rows(narrow(dot(outer, left)), inner)
        turn_ref[...] = narrow(jnp.where(at(big, 0) // rows == at(big, 1) // rows, turn, 0.0))
        mix_ref[...] = narrow(jnp.where(at(big, 0) % GROUP == at(big, 1) // rows, mix, 0.0))
        right = right_ref[...]
        pair_ref[...] = jnp.zeros_like(pair_ref)
        pair_ref[:cols, :cols] = right
        pair_ref[cols:, cols:] = right
        eig = eig_ref[...].astype(jnp.float32)
        summed = jnp.sum(jnp.where(at(eig.shape, 0) < live, eig, 0.0))
        damping = 0.1 * summed / jnp.maximum(live * cols, 1).astype(jnp.float32)
        inverse = jnp.broadcast_to((1.0 / (eig + damping))[None], (GROUP, rows, cols))
        inverse = inverse.reshape(span, cols)
        inv_ref[...] = jnp.concatenate([inverse, inverse], 1)
        turn, mix, pair, inverse = turn_ref[...], mix_ref[...], pair_ref[...], inv_ref[...]
        for two in range(block // (2 * GROUP)):
            first, second = (
                train_ref[(2 * two + k) * GROUP : (2 * two + k + 1) * GROUP].reshape(span, cols)
                for k in range(2)
            )
            value = dot(jnp.concatenate([first, second], 1), pair)
            value = mixed_by(turn, value, REFINED[0]) * inverse
            if REFINED[1]:
                high, low = halves(value)
                value = dot_by_rows(high, pair) + dot_by_rows(low, pair)
            else:
                value = dot_by_rows(narrow(value), pair)
            value = narrow(mixed_by(mix, value, REFINED[2]))
            for k in range(2):
                base = (2 * two + k) * GROUP
                for row in range(rows):
                    out_ref[base : base + GROUP, row * cols : (row + 1) * cols] = value[
                        row * GROUP : (row + 1) * GROUP, k * cols : (k + 1) * cols
                    ]


def preconditioned_train(live, train_grads, left, right, eigenvalues, part, parts):
    count, slots, rows, cols = train_grads.shape
    block = count // parts
    span = GROUP * rows
    per_slot = lambda *shape: pl.BlockSpec((None, *shape), lambda s, live: (s, 0, 0))
    return pl.pallas_call(
        train_kernel,
        grid_spec=pltpu.PrefetchScalarGridSpec(
            num_scalar_prefetch=1,
            grid=(slots,),
            in_specs=[
                pl.BlockSpec((block, None, rows, cols), lambda s, live: (part, s, 0, 0)),
                per_slot(rows, rows),
                per_slot(cols, cols),
                per_slot(rows, cols),
            ],
            out_specs=pl.BlockSpec((block, rows * cols), lambda s, live: (0, s)),
            scratch_shapes=[
                pltpu.VMEM((span, span), jnp.bfloat16),
                pltpu.VMEM((span, span), jnp.bfloat16),
                pltpu.VMEM((2 * cols, 2 * cols), jnp.bfloat16),
                pltpu.VMEM((span, 2 * cols), jnp.float32),
            ],
        ),
        out_shape=jax.ShapeDtypeStruct((block, slots * rows * cols), jnp.bfloat16),
        cost_estimate=pl.CostEstimate(
            flops=8 * block * slots * rows * cols * span, bytes_accessed=1 << 23, transcendentals=0
        ),
    )(live, train_grads, left, right, eigenvalues)


def score_kernel(side_ref, query_ref, *refs):
    train_refs, (out_ref, sort_ref, flat_ref, sum_ref) = refs[:-4], refs[-4:]
    parts = len(train_refs) // 2
    count, rows, cols = query_ref.shape
    span = GROUP * rows
    step, last = pl.program_id(0), pl.num_programs(0) - 1
    block = train_refs[0].shape[0]

    @pl.when(step == 0)
    def _():
        to = lax.broadcasted_iota(jnp.int32, (span, span), 0)
        of = lax.broadcasted_iota(jnp.int32, (span, span), 1)
        same = (to % GROUP == of // rows) & (to // GROUP == of % rows)
        sort_ref[...] = same.astype(jnp.float32).astype(jnp.bfloat16)

    sort = sort_ref[...]
    for two in range(count // (2 * GROUP)):
        first, second = (
            query_ref[(2 * two + k) * GROUP : (2 * two + k + 1) * GROUP].reshape(span, cols)
            for k in range(2)
        )
        ordered = dot(sort, jnp.concatenate([first, second], 1)).astype(jnp.bfloat16)
        for k in range(2):
            base = (2 * two + k) * GROUP
            for row in range(rows):
                flat_ref[base : base + GROUP, row * cols : (row + 1) * cols] = ordered[
                    row * GROUP : (row + 1) * GROUP, k * cols : (k + 1) * cols
                ]
    flat = flat_ref[...]
    for index, train_ref in enumerate(train_refs):
        part = dot_by_rows(flat, train_ref[...])
        at = (index // parts, slice(None), pl.ds(index % parts * block, block))

        @pl.when(step == 0)
        def _():
            sum_ref[at] = part

        @pl.when(step > 0)
        def _():
            sum_ref[at] += part

    @pl.when(step == last)
    def _():
        side = side_ref[0]
        out_ref[side] = sum_ref[0].astype(out_ref.dtype)
        out_ref[1 - side] = sum_ref[1].astype(out_ref.dtype)


def scores(side, queries, train_parts):
    count, slots, rows, cols = queries.shape
    block = train_parts[0].shape[0]
    train_count = block * len(train_parts) // 2
    span = GROUP * rows
    flat = pl.BlockSpec((block, rows * cols), lambda s, side: (0, s))
    return pl.pallas_call(
        score_kernel,
        grid_spec=pltpu.PrefetchScalarGridSpec(
            num_scalar_prefetch=1,
            grid=(slots,),
            in_specs=[pl.BlockSpec((count, None, rows, cols), lambda s, side: (0, s, 0, 0))]
            + [flat] * len(train_parts),
            out_specs=pl.BlockSpec((2, count, train_count), lambda s, side: (0, 0, 0)),
            scratch_shapes=[
                pltpu.VMEM((span, span), jnp.bfloat16),
                pltpu.VMEM((count, rows * cols), jnp.bfloat16),
                pltpu.VMEM((2, count, train_count), jnp.float32),
            ],
        ),
        out_shape=jax.ShapeDtypeStruct((2, count, train_count), jnp.bfloat16),
        cost_estimate=pl.CostEstimate(
            flops=4 * count * train_count * slots * rows * cols, bytes_accessed=1 << 24, transcendentals=0
        ),
        name="scores",
    )(side, queries, *train_parts)


def on_device(query_grads, train_grads, left_basis, right_basis, eigenvalues, block_rows):
    per_source, slot_total, rows, cols = query_grads.shape
    owners = lax.axis_size("mod")
    slots = slot_total // owners
    norm_scale = 1.0 / math.sqrt(slot_total * rows * cols)

    sent = by_owner(query_grads, owners)
    got = lax.all_to_all(sent, "mod", split_axis=0, concat_axis=0, tiled=True)
    got = got.reshape(owners * per_source, slots, rows, cols)

    parts = 2
    own = [
        preconditioned_train(
            block_rows, train_grads, left_basis, right_basis, eigenvalues, k, parts
        )
        for k in range(parts)
    ]
    far = [lax.ppermute(value, "pair", [(0, 1), (1, 0)]) for value in own]
    side = lax.axis_index("pair").astype(jnp.int32).reshape(1)
    partial = scores(side, got, own + far)
    partial = jnp.swapaxes(partial.reshape(2, owners, per_source, -1), 0, 1)
    partial = partial.reshape(2 * owners, per_source, -1)
    back = lax.all_to_all(partial, ("mod", "pair"), split_axis=0, concat_axis=0, tiled=True)
    back = back.reshape(owners, 2 * per_source, -1)
    return jnp.sum(back.astype(jnp.float32), 0) * norm_scale


def solution(mesh):
    placed = (
        P(("mod", "pair"), None, None, None),
        P("pair", "mod", None, None),
        P("mod", None, None),
        P("mod", None, None),
        P("mod", None, None),
        P("mod"),
    )
    return jax.shard_map(
        on_device, mesh=mesh, in_specs=placed, out_specs=P("mod", "pair"), check_vma=False
    )
```

```python
import functools
import math

import jax
import jax.numpy as jnp
from jax import lax
from jax.experimental import pallas as pl
from jax.experimental.pallas import tpu as pltpu
from jax.sharding import PartitionSpec as P


GROUP = 16
REFINED = (True, False, True)


def dot(a, b):
    return jnp.dot(a, b, preferred_element_type=jnp.float32)


def dot_by_rows(a, b):
    return lax.dot_general(a, b, (((1,), (1,)), ((), ())), preferred_element_type=jnp.float32)


def halves(value):
    high = value.astype(jnp.bfloat16)
    return high, (value - high.astype(jnp.float32)).astype(jnp.bfloat16)


def mixed_by(matrix, value, refined):
    if not refined:
        return dot(matrix, value.astype(jnp.bfloat16))
    high, low = halves(value)
    return dot(matrix, high) + dot(matrix, low)


def arrange_kernel(in_ref, out_ref, held_ref, in_sem, out_sem):
    queries = range(in_ref.shape[0])
    fetch = [
        pltpu.make_async_copy(in_ref.at[q], held_ref.at[q], in_sem.at[q]) for q in queries
    ]
    place = [
        pltpu.make_async_copy(held_ref.at[q], out_ref.at[:, q], out_sem.at[q]) for q in queries
    ]
    for copy in fetch:
        copy.start()
    for q in queries:
        fetch[q].wait()
        place[q].start()
    for copy in place:
        copy.wait()


def by_owner(query_grads, owners):
    count, slot_total, rows, cols = query_grads.shape
    slots = slot_total // owners
    shape = (count, owners, slots, rows, cols)
    return pl.pallas_call(
        arrange_kernel,
        in_specs=[pl.BlockSpec(memory_space=pl.ANY)],
        out_specs=pl.BlockSpec(memory_space=pl.ANY),
        out_shape=jax.ShapeDtypeStruct((owners, count, slots, rows, cols), query_grads.dtype),
        scratch_shapes=[
            pltpu.VMEM(shape, query_grads.dtype),
            pltpu.SemaphoreType.DMA((count,)),
            pltpu.SemaphoreType.DMA((count,)),
        ],
        name="by_owner",
    )(query_grads.reshape(shape))


def train_kernel(
    live_ref, train_ref, left_ref, right_ref, eig_ref, out_ref, turn_ref, mix_ref, pair_ref, inv_ref,
    *, first_slot
):
    block, rows, cols = train_ref.shape
    span = GROUP * rows
    live = live_ref[first_slot + pl.program_id(0)]

    @pl.when(live == 0)
    def _():
        out_ref[...] = jnp.zeros_like(out_ref)

    @pl.when((live > 0) & (pl.program_id(1) == 0))
    def _():
        at = lambda shape, axis: lax.broadcasted_iota(jnp.int32, shape, axis)
        square = (rows, rows)
        kept = (at(square, 0) < live) & (at(square, 1) < live)
        left = jnp.where(kept, left_ref[...].astype(jnp.float32), 0.0).astype(jnp.bfloat16)
        tall, big = (span, rows), (span, span)
        ones = lambda mask: mask.astype(jnp.float32).astype(jnp.bfloat16)
        inner = ones(at(tall, 0) % rows == at(tall, 1))
        outer = ones(at(tall, 0) // GROUP == at(tall, 1))
        narrow = lambda value: value.astype(jnp.bfloat16)
        turn = dot_by_rows(narrow(dot_by_rows(inner, left)), inner)
        mix = dot_by_rows(narrow(dot(outer, left)), inner)
        turn_ref[...] = narrow(jnp.where(at(big, 0) // rows == at(big, 1) // rows, turn, 0.0))
        mix_ref[...] = narrow(jnp.where(at(big, 0) % GROUP == at(big, 1) // rows, mix, 0.0))
        right = right_ref[...]
        pair_ref[...] = jnp.zeros_like(pair_ref)
        pair_ref[:cols, :cols] = right
        pair_ref[cols:, cols:] = right
        eig = eig_ref[...].astype(jnp.float32)
        summed = jnp.sum(jnp.where(at(eig.shape, 0) < live, eig, 0.0))
        damping = 0.1 * summed / jnp.maximum(live * cols, 1).astype(jnp.float32)
        inverse = jnp.broadcast_to((1.0 / (eig + damping))[None], (GROUP, rows, cols))
        inverse = inverse.reshape(span, cols)
        inv_ref[...] = jnp.concatenate([inverse, inverse], 1)

    @pl.when(live > 0)
    def _():
        turn, mix, pair, inverse = turn_ref[...], mix_ref[...], pair_ref[...], inv_ref[...]
        for two in range(block // (2 * GROUP)):
            first, second = (
                train_ref[(2 * two + k) * GROUP : (2 * two + k + 1) * GROUP].reshape(span, cols)
                for k in range(2)
            )
            value = dot(jnp.concatenate([first, second], 1), pair)
            value = mixed_by(turn, value, REFINED[0]) * inverse
            if REFINED[1]:
                high, low = halves(value)
                value = dot_by_rows(high, pair) + dot_by_rows(low, pair)
            else:
                value = dot_by_rows(value.astype(jnp.bfloat16), pair)
            value = mixed_by(mix, value, REFINED[2]).astype(jnp.bfloat16)
            for k in range(2):
                base = (2 * two + k) * GROUP
                for row in range(rows):
                    out_ref[base : base + GROUP, row * cols : (row + 1) * cols] = value[
                        row * GROUP : (row + 1) * GROUP, k * cols : (k + 1) * cols
                    ]


def preconditioned_train(live, train_grads, left, right, eigenvalues, part, parts, block):
    count, slots, rows, cols = train_grads.shape
    here = slots // parts
    span = GROUP * rows
    per_slot = lambda *shape: pl.BlockSpec((None, *shape), lambda s, i, live: (part * here + s, 0, 0))
    return pl.pallas_call(
        functools.partial(train_kernel, first_slot=part * here),
        grid_spec=pltpu.PrefetchScalarGridSpec(
            num_scalar_prefetch=1,
            grid=(here, count // block),
            in_specs=[
                pl.BlockSpec((block, None, rows, cols), lambda s, i, live: (i, part * here + s, 0, 0)),
                per_slot(rows, rows),
                per_slot(cols, cols),
                per_slot(rows, cols),
            ],
            out_specs=pl.BlockSpec((block, rows * cols), lambda s, i, live: (i, s)),
            scratch_shapes=[
                pltpu.VMEM((span, span), jnp.bfloat16),
                pltpu.VMEM((span, span), jnp.bfloat16),
                pltpu.VMEM((2 * cols, 2 * cols), jnp.bfloat16),
                pltpu.VMEM((span, 2 * cols), jnp.float32),
            ],
        ),
        out_shape=jax.ShapeDtypeStruct((count, here * rows * cols), jnp.bfloat16),
        cost_estimate=pl.CostEstimate(
            flops=8 * count * here * rows * cols * span, bytes_accessed=1 << 23, transcendentals=0
        ),
    )(live, train_grads, left, right, eigenvalues)


def score_kernel(side_ref, query_ref, *refs, slots_per_part):
    train_refs, refs = refs[:-7], refs[-7:]
    out_ref, query_buf, train_buf, flat_ref, sum_ref, query_sem, train_sem = refs
    slots, count, rows, cols = query_buf.shape
    width = rows * cols
    pieces = 2
    block = train_buf.shape[2]

    def query_copy(slot):
        return pltpu.make_async_copy(
            query_ref.at[:, slot], query_buf.at[slot], query_sem.at[slot]
        )

    def train_copy(slot, piece):
        part, place = divmod(slot, slots_per_part)
        source = train_refs[piece * (len(train_refs) // pieces) + part]
        return pltpu.make_async_copy(
            source.at[:, pl.ds(place * width, width)],
            train_buf.at[slot, piece],
            train_sem.at[slot, piece],
        )

    def fetch(slot):
        query_copy(slot).start()
        for piece in range(pieces):
            train_copy(slot, piece).start()

    fetch(0)
    for slot in range(slots):
        query_copy(slot).wait()
        if slot + 1 < slots:
            fetch(slot + 1)
        for group in range(count // GROUP):
            base = group * GROUP
            ordered = jnp.swapaxes(query_buf[slot, base : base + GROUP], 0, 1)
            for row in range(rows):
                flat_ref[slot % 2, base : base + GROUP, row * cols : (row + 1) * cols] = ordered[row]
        for piece in range(pieces):
            train_copy(slot, piece).wait()
            part = dot_by_rows(flat_ref[slot % 2], train_buf[slot, piece])
            if slot == 0:
                sum_ref[piece] = part
            else:
                sum_ref[piece] += part
    side = side_ref[0]
    lower = lax.broadcasted_iota(jnp.int32, (count, cols), 0) % 8 < 4
    for piece in range(pieces):
        even, odd = [], []
        for pair in range(block // (2 * cols)):
            a = sum_ref[piece, :, 2 * pair * cols : (2 * pair + 1) * cols]
            b = sum_ref[piece, :, (2 * pair + 1) * cols : (2 * pair + 2) * cols]
            even.append(jnp.where(lower, a, pltpu.roll(b, 4, 0)).reshape(count // 8, 8, cols))
            odd.append(jnp.where(lower, pltpu.roll(a, count - 4, 0), b).reshape(count // 8, 8, cols))
        place = side if piece == 0 else 1 - side
        out_ref[:, 0, place] = jnp.concatenate(even, 1).astype(out_ref.dtype)
        out_ref[:, 1, place] = jnp.concatenate(odd, 1).astype(out_ref.dtype)


def scores(side, queries, train_parts):
    count, slots, rows, cols = queries.shape
    block = train_parts[0].shape[0]
    width = rows * cols
    whole = pl.BlockSpec(memory_space=pltpu.HBM)
    out = jax.ShapeDtypeStruct((count // 8, 2, 2, 4 * block // cols, cols), jnp.bfloat16)
    return pl.pallas_call(
        functools.partial(score_kernel, slots_per_part=2 * slots // len(train_parts)),
        in_specs=[pl.BlockSpec(memory_space=pltpu.SMEM)] + [whole] * (1 + len(train_parts)),
        out_shape=out,
        scratch_shapes=[
            pltpu.VMEM((slots, count, rows, cols), jnp.bfloat16),
            pltpu.VMEM((slots, 2, block, width), jnp.bfloat16),
            pltpu.VMEM((2, count, width), jnp.bfloat16),
            pltpu.VMEM((2, count, block), jnp.float32),
            pltpu.SemaphoreType.DMA((slots,)),
            pltpu.SemaphoreType.DMA((slots, 2)),
        ],
        cost_estimate=pl.CostEstimate(
            flops=4 * count * block * slots * width, bytes_accessed=1 << 24, transcendentals=0
        ),
        compiler_params=pltpu.CompilerParams(vmem_limit_bytes=50 << 20),
        name="scores",
    )(side, queries, *train_parts)


def total_kernel(part_ref, out_ref, *, scale):
    summed = jnp.sum(part_ref[...].astype(jnp.float32), 0) * scale
    sides, height, cols = summed.shape
    for side in range(sides):
        for tile in range(height // 4):
            out_ref[side * 4 : side * 4 + 4, tile * cols : (tile + 1) * cols] = summed[
                side, tile * 4 : tile * 4 + 4
            ]


def total(parts, scale):
    _, sides, height, cols = parts.shape
    return pl.pallas_call(
        functools.partial(total_kernel, scale=scale),
        out_shape=jax.ShapeDtypeStruct((4 * sides, height // 4 * cols), jnp.float32),
        compiler_params=pltpu.CompilerParams(vmem_limit_bytes=4 << 20),
        name="total",
    )(parts)


def on_device(query_grads, train_grads, left_basis, right_basis, eigenvalues, block_rows):
    per_source, slot_total, rows, cols = query_grads.shape
    owners = lax.axis_size("mod")
    slots = slot_total // owners
    norm_scale = 1.0 / math.sqrt(slot_total * rows * cols)

    sent = by_owner(query_grads, owners)
    got = lax.all_to_all(sent, "mod", split_axis=0, concat_axis=0, tiled=True)
    got = got.reshape(owners * per_source, slots, rows, cols)

    parts = 2
    own = [
        preconditioned_train(
            block_rows, train_grads, left_basis, right_basis, eigenvalues, k, parts, 256
        )
        for k in range(parts)
    ]
    far = [lax.ppermute(value, "pair", [(0, 1), (1, 0)]) for value in own]
    side = lax.axis_index("pair").astype(jnp.int32).reshape(1)
    partial = scores(side, got, own + far)
    partial = partial.reshape(2 * owners, *partial.shape[3:])
    back = lax.all_to_all(partial, ("mod", "pair"), split_axis=0, concat_axis=0, tiled=True)
    return total(back.reshape(owners, 2, *back.shape[1:]), norm_scale)


def solution(mesh):
    placed = (
        P(("mod", "pair"), None, None, None),
        P("pair", "mod", None, None),
        P("mod", None, None),
        P("mod", None, None),
        P("mod", None, None),
        P("mod"),
    )
    return jax.shard_map(
        on_device, mesh=mesh, in_specs=placed, out_specs=P("mod", "pair"), check_vma=False
    )
```

```python
import functools
import math

import jax
import jax.numpy as jnp
from jax import lax
from jax.experimental import pallas as pl
from jax.experimental.pallas import tpu as pltpu
from jax.sharding import PartitionSpec as P


GROUP = 16
REFINED = (True, False, True)


def dot(a, b):
    return jnp.dot(a, b, preferred_element_type=jnp.float32)


def dot_by_rows(a, b):
    return lax.dot_general(a, b, (((1,), (1,)), ((), ())), preferred_element_type=jnp.float32)


def halves(value):
    high = value.astype(jnp.bfloat16)
    return high, (value - high.astype(jnp.float32)).astype(jnp.bfloat16)


def mixed_by(matrix, value, refined):
    if not refined:
        return dot(matrix, value.astype(jnp.bfloat16))
    high, low = halves(value)
    return dot(matrix, high) + dot(matrix, low)


def arrange_kernel(in_ref, out_ref, held_ref, in_sem, out_sem):
    queries = range(in_ref.shape[0])
    fetch = [
        pltpu.make_async_copy(in_ref.at[q], held_ref.at[q], in_sem.at[q]) for q in queries
    ]
    place = [
        pltpu.make_async_copy(held_ref.at[q], out_ref.at[:, q], out_sem.at[q]) for q in queries
    ]
    for copy in fetch:
        copy.start()
    for q in queries:
        fetch[q].wait()
        place[q].start()
    for copy in place:
        copy.wait()


def by_owner(query_grads, owners):
    count, slot_total, rows, cols = query_grads.shape
    slots = slot_total // owners
    shape = (count, owners, slots, rows, cols)
    return pl.pallas_call(
        arrange_kernel,
        in_specs=[pl.BlockSpec(memory_space=pl.ANY)],
        out_specs=pl.BlockSpec(memory_space=pl.ANY),
        out_shape=jax.ShapeDtypeStruct((owners, count, slots, rows, cols), query_grads.dtype),
        scratch_shapes=[
            pltpu.VMEM(shape, query_grads.dtype),
            pltpu.SemaphoreType.DMA((count,)),
            pltpu.SemaphoreType.DMA((count,)),
        ],
        name="by_owner",
    )(query_grads.reshape(shape))


def train_kernel(
    live_ref, train_ref, left_ref, right_ref, eig_ref, out_ref, turn_ref, mix_ref, pair_ref, inv_ref,
    *, first_slot
):
    block, rows, cols = train_ref.shape
    span = GROUP * rows
    live = live_ref[first_slot + pl.program_id(0)]

    @pl.when(live == 0)
    def _():
        out_ref[...] = jnp.zeros_like(out_ref)

    @pl.when((live > 0) & (pl.program_id(1) == 0))
    def _():
        at = lambda shape, axis: lax.broadcasted_iota(jnp.int32, shape, axis)
        square = (rows, rows)
        kept = (at(square, 0) < live) & (at(square, 1) < live)
        left = jnp.where(kept, left_ref[...].astype(jnp.float32), 0.0).astype(jnp.bfloat16)
        tall, big = (span, rows), (span, span)
        ones = lambda mask: mask.astype(jnp.float32).astype(jnp.bfloat16)
        inner = ones(at(tall, 0) % rows == at(tall, 1))
        outer = ones(at(tall, 0) // GROUP == at(tall, 1))
        narrow = lambda value: value.astype(jnp.bfloat16)
        turn = dot_by_rows(narrow(dot_by_rows(inner, left)), inner)
        mix = dot_by_rows(narrow(dot(outer, left)), inner)
        turn_ref[...] = narrow(jnp.where(at(big, 0) // rows == at(big, 1) // rows, turn, 0.0))
        mix_ref[...] = narrow(jnp.where(at(big, 0) % GROUP == at(big, 1) // rows, mix, 0.0))
        right = right_ref[...]
        pair_ref[...] = jnp.zeros_like(pair_ref)
        pair_ref[:cols, :cols] = right
        pair_ref[cols:, cols:] = right
        eig = eig_ref[...].astype(jnp.float32)
        summed = jnp.sum(jnp.where(at(eig.shape, 0) < live, eig, 0.0))
        damping = 0.1 * summed / jnp.maximum(live * cols, 1).astype(jnp.float32)
        inverse = jnp.broadcast_to((1.0 / (eig + damping))[None], (GROUP, rows, cols))
        inverse = inverse.reshape(span, cols)
        inv_ref[...] = jnp.concatenate([inverse, inverse], 1)

    @pl.when(live > 0)
    def _():
        turn, mix, pair, inverse = turn_ref[...], mix_ref[...], pair_ref[...], inv_ref[...]
        for two in range(block // (2 * GROUP)):
            first, second = (
                train_ref[(2 * two + k) * GROUP : (2 * two + k + 1) * GROUP].reshape(span, cols)
                for k in range(2)
            )
            value = dot(jnp.concatenate([first, second], 1), pair)
            value = mixed_by(turn, value, REFINED[0]) * inverse
            if REFINED[1]:
                high, low = halves(value)
                value = dot_by_rows(high, pair) + dot_by_rows(low, pair)
            else:
                value = dot_by_rows(value.astype(jnp.bfloat16), pair)
            value = mixed_by(mix, value, REFINED[2]).astype(jnp.bfloat16)
            for k in range(2):
                base = (2 * two + k) * GROUP
                for row in range(rows):
                    out_ref[base : base + GROUP, row * cols : (row + 1) * cols] = value[
                        row * GROUP : (row + 1) * GROUP, k * cols : (k + 1) * cols
                    ]


def preconditioned_train(live, train_grads, left, right, eigenvalues, part, parts, block):
    count, slots, rows, cols = train_grads.shape
    here = slots // parts
    span = GROUP * rows
    per_slot = lambda *shape: pl.BlockSpec((None, *shape), lambda s, i, live: (part * here + s, 0, 0))
    return pl.pallas_call(
        functools.partial(train_kernel, first_slot=part * here),
        grid_spec=pltpu.PrefetchScalarGridSpec(
            num_scalar_prefetch=1,
            grid=(here, count // block),
            in_specs=[
                pl.BlockSpec((block, None, rows, cols), lambda s, i, live: (i, part * here + s, 0, 0)),
                per_slot(rows, rows),
                per_slot(cols, cols),
                per_slot(rows, cols),
            ],
            out_specs=pl.BlockSpec((block, rows * cols), lambda s, i, live: (i, s)),
            scratch_shapes=[
                pltpu.VMEM((span, span), jnp.bfloat16),
                pltpu.VMEM((span, span), jnp.bfloat16),
                pltpu.VMEM((2 * cols, 2 * cols), jnp.bfloat16),
                pltpu.VMEM((span, 2 * cols), jnp.float32),
            ],
        ),
        out_shape=jax.ShapeDtypeStruct((count, here * rows * cols), jnp.bfloat16),
        cost_estimate=pl.CostEstimate(
            flops=8 * count * here * rows * cols * span, bytes_accessed=1 << 23, transcendentals=0
        ),
    )(live, train_grads, left, right, eigenvalues)


def score_kernel(side_ref, query_ref, *refs, slots_per_part):
    train_refs, refs = refs[:-7], refs[-7:]
    out_ref, query_buf, train_buf, flat_ref, sum_ref, query_sem, train_sem = refs
    slots, count, rows, cols = query_buf.shape
    width = rows * cols
    pieces = 2
    block = train_buf.shape[2]

    def query_copy(slot):
        return pltpu.make_async_copy(
            query_ref.at[:, slot], query_buf.at[slot], query_sem.at[slot]
        )

    def train_copy(slot, piece):
        part, place = divmod(slot, slots_per_part)
        source = train_refs[piece * (len(train_refs) // pieces) + part]
        return pltpu.make_async_copy(
            source.at[:, pl.ds(place * width, width)],
            train_buf.at[slot, piece],
            train_sem.at[slot, piece],
        )

    def fetch(slot):
        query_copy(slot).start()
        for piece in range(pieces):
            train_copy(slot, piece).start()

    fetch(0)
    fetch(1)
    for slot in range(slots):
        query_copy(slot).wait()
        if slot == 0:
            for later in range(2, slots):
                fetch(later)
        for group in range(count // GROUP):
            base = group * GROUP
            ordered = jnp.swapaxes(query_buf[slot, base : base + GROUP], 0, 1)
            for row in range(rows):
                flat_ref[slot % 2, base : base + GROUP, row * cols : (row + 1) * cols] = ordered[row]
        for piece in range(pieces):
            train_copy(slot, piece).wait()
            part = dot_by_rows(flat_ref[slot % 2], train_buf[slot, piece])
            if slot == 0:
                sum_ref[piece] = part
            else:
                sum_ref[piece] += part
    side = side_ref[0]
    lower = lax.broadcasted_iota(jnp.int32, (count, cols), 0) % 8 < 4
    for piece in range(pieces):
        even, odd = [], []
        for pair in range(block // (2 * cols)):
            a = sum_ref[piece, :, 2 * pair * cols : (2 * pair + 1) * cols]
            b = sum_ref[piece, :, (2 * pair + 1) * cols : (2 * pair + 2) * cols]
            even.append(jnp.where(lower, a, pltpu.roll(b, 4, 0)).reshape(count // 8, 8, cols))
            odd.append(jnp.where(lower, pltpu.roll(a, count - 4, 0), b).reshape(count // 8, 8, cols))
        place = side if piece == 0 else 1 - side
        out_ref[:, 0, place] = jnp.concatenate(even, 1).astype(out_ref.dtype)
        out_ref[:, 1, place] = jnp.concatenate(odd, 1).astype(out_ref.dtype)


def scores(side, queries, train_parts):
    count, slots, rows, cols = queries.shape
    block = train_parts[0].shape[0]
    width = rows * cols
    whole = pl.BlockSpec(memory_space=pltpu.HBM)
    out = jax.ShapeDtypeStruct((count // 8, 2, 2, 4 * block // cols, cols), jnp.bfloat16)
    return pl.pallas_call(
        functools.partial(score_kernel, slots_per_part=2 * slots // len(train_parts)),
        in_specs=[pl.BlockSpec(memory_space=pltpu.SMEM)] + [whole] * (1 + len(train_parts)),
        out_shape=out,
        scratch_shapes=[
            pltpu.VMEM((slots, count, rows, cols), jnp.bfloat16),
            pltpu.VMEM((slots, 2, block, width), jnp.bfloat16),
            pltpu.VMEM((2, count, width), jnp.bfloat16),
            pltpu.VMEM((2, count, block), jnp.float32),
            pltpu.SemaphoreType.DMA((slots,)),
            pltpu.SemaphoreType.DMA((slots, 2)),
        ],
        cost_estimate=pl.CostEstimate(
            flops=4 * count * block * slots * width, bytes_accessed=1 << 24, transcendentals=0
        ),
        compiler_params=pltpu.CompilerParams(vmem_limit_bytes=50 << 20),
        name="scores",
    )(side, queries, *train_parts)


def total_kernel(part_ref, out_ref, *, scale):
    summed = jnp.sum(part_ref[...].astype(jnp.float32), 0) * scale
    sides, height, cols = summed.shape
    for side in range(sides):
        for tile in range(height // 4):
            out_ref[side * 4 : side * 4 + 4, tile * cols : (tile + 1) * cols] = summed[
                side, tile * 4 : tile * 4 + 4
            ]


def total(parts, scale):
    _, sides, height, cols = parts.shape
    return pl.pallas_call(
        functools.partial(total_kernel, scale=scale),
        out_shape=jax.ShapeDtypeStruct((4 * sides, height // 4 * cols), jnp.float32),
        compiler_params=pltpu.CompilerParams(vmem_limit_bytes=4 << 20),
        name="total",
    )(parts)


def on_device(query_grads, train_grads, left_basis, right_basis, eigenvalues, block_rows):
    per_source, slot_total, rows, cols = query_grads.shape
    owners = lax.axis_size("mod")
    slots = slot_total // owners
    norm_scale = 1.0 / math.sqrt(slot_total * rows * cols)

    sent = by_owner(query_grads, owners)
    got = lax.all_to_all(sent, "mod", split_axis=0, concat_axis=0, tiled=True)
    got = got.reshape(owners * per_source, slots, rows, cols)

    parts = 4
    own = [
        preconditioned_train(
            block_rows, train_grads, left_basis, right_basis, eigenvalues, k, parts, 256
        )
        for k in range(parts)
    ]
    far = [lax.ppermute(value, "pair", [(0, 1), (1, 0)]) for value in own]
    side = lax.axis_index("pair").astype(jnp.int32).reshape(1)
    partial = scores(side, got, own + far)
    partial = partial.reshape(2 * owners, *partial.shape[3:])
    back = lax.all_to_all(partial, ("mod", "pair"), split_axis=0, concat_axis=0, tiled=True)
    return total(back.reshape(owners, 2, *back.shape[1:]), norm_scale)


def solution(mesh):
    placed = (
        P(("mod", "pair"), None, None, None),
        P("pair", "mod", None, None),
        P("mod", None, None),
        P("mod", None, None),
        P("mod", None, None),
        P("mod"),
    )
    return jax.shard_map(
        on_device, mesh=mesh, in_specs=placed, out_specs=P("mod", "pair"), check_vma=False
    )
```
